32 devices in a mesh: tm: 16 (over z, x, core), space: 2 (over y).
Axes of the slice: x: 2, y: 2, z: 4, core: 2. Of those that a mesh axis runs over, the one named last changes fastest.
Arguments:
- trajectory: bfloat16 [64, 64, 1024], P('tm', 'space'), may hold values from 0.19921875 to 0.8984375
- target: float32 [64, 1024], P('space'), may hold values from -6 to 6
- reaction: float32 [64, 1024], P('space'), may hold values from 0.0078125 to 0.3125
- guess: float32 [16, 64, 1024], P('tm', 'space'), may hold values from -6 to 6
Outputs:
- adjoint: float32 [64, 64, 1024], P('tm', 'space')
The draws below stay inside these ranges and needn't reach their ends.
All inputs are finite; a program needn't handle non-finite values.
Results may differ from the reference program's by a relative error of at most 0.0003.
Values sent between devices are 32-bit elements; how exact they have to be, the bound alone decides.
A program may use at most 64 MiB of HBM per device.

```python
import math
import jax
import jax.numpy as jnp
from jax import lax

NY = 1024
M = 4
NX = 64
NT = 64
NC = 16


def levels(key, shape, cuts, low, high):
    def one(position, parts):
        draws = jax.random.uniform(jax.random.fold_in(jax.random.fold_in(key, 6), position), (parts,), jnp.float32, low / len(cuts), high / len(cuts))
        return jnp.repeat(jnp.exp(draws), shape[position] // parts).reshape((-1,) + (1,) * (len(shape) - position - 1))

    factor_of = one(*cuts[0])
    for cut in cuts[1:]:
        factor_of = factor_of * one(*cut)
    return factor_of


def scatter_about(own_key, shape, deviation, bound, split=(), held_as=jnp.bfloat16):
    gain = levels(own_key, shape, split, -0.22, 0.18) if split else 1.0
    entries = jax.random.normal(own_key, shape, jnp.float32) * deviation * gain
    return jnp.minimum(jnp.maximum(entries, -bound), bound).astype(held_as)


def setup_inputs(seed: int = 0) -> dict:
    splits = jax.random.split(jax.random.key(seed), 5)
    trajectory = jnp.clip(0.19921875 + 0.69921875 * jax.random.uniform(splits[0], (NT, NX, NY), jnp.float32) ** levels(splits[0], (NT, NX, NY), ((0, 16), (1, 2)), -0.2, 0.2), 0.19921875, 0.8984375).astype(jnp.bfloat16)
    target = scatter_about(splits[1], (NX, NY), 1.0, 6.0, ((0, 2),), jnp.float32)
    reaction = jnp.clip(jnp.exp(math.log(0.3125) - 3.6888795 * jax.random.uniform(splits[2], (NX, NY), jnp.float32) ** levels(splits[2], (NX, NY), ((0, 2),), -0.2, 0.2)), 0.0078125, 0.3125)
    guess = scatter_about(splits[3], (NC, NX, NY), 1.0, 6.0, ((0, 16), (1, 2)), jnp.float32)
    return {"trajectory": trajectory, "target": target, "reaction": reaction, "guess": guess}


DIFFUSION = 0.05


def advance(field, rate_field, source_field):
    padded = jnp.pad(field, ((0, 0), (1, 1), (1, 1)))
    neighbours = padded[:, :-2, 1:-1] + padded[:, 2:, 1:-1]
    neighbours = neighbours + padded[:, 1:-1, :-2] + padded[:, 1:-1, 2:]
    return field + DIFFUSION * (neighbours - 4.0 * field) + rate_field * field + source_field


def reference(trajectory, target, reaction, guess):
    trajectory_blocks = trajectory.astype(jnp.float32).reshape(NC, M, NX, NY)

    def rate_at(i):
        return reaction[None] * (1.0 - 2.0 * trajectory_blocks[:, i])

    def source_at(i):
        return (trajectory_blocks[:, i] - target[None]) / float(NT)

    def relaxation(cvalues):
        field = jnp.concatenate([cvalues[1:], jnp.zeros_like(cvalues[:1])], 0)
        fine_vals = {}
        for i in range(M - 1, 0, -1):
            field = advance(field, rate_at(i), source_at(i))
            fine_vals[i] = field
        return fine_vals

    coarse_rate = jnp.ones_like(guess)
    for i in range(M):
        coarse_rate = coarse_rate * (1.0 + rate_at(i))
    fine_vals = relaxation(guess)
    cvalues = advance(fine_vals[1], rate_at(0), source_at(0))
    fine_vals = relaxation(cvalues)
    residual = advance(fine_vals[1], rate_at(0), source_at(0)) - cvalues

    def backward(running, inputs):
        factor_j, residual_j = inputs
        running = factor_j * running + residual_j
        return running, running

    start = jnp.zeros((NX, NY), jnp.float32)
    _, correction = lax.scan(backward, start, (coarse_rate, residual), reverse=True)
    cvalues = cvalues + correction
    fine_vals = relaxation(cvalues)
    stacked = jnp.stack([cvalues] + [fine_vals[i] for i in range(1, M)], axis=1)
    return stacked.reshape(NT, NX, NY)
```

```python
import functools
import jax
import jax.numpy as jnp
from jax import lax
from jax.experimental import pallas as pl
from jax.experimental.pallas import tpu as pltpu
from jax.sharding import PartitionSpec as P

DIFFUSION = 0.05
MESH = pl.DeviceIdType.MESH
EDGE = 8


def group_size(count, cols):
    best = 1
    for d in range(1, count + 1):
        if d * d <= count and count % d == 0 and cols % (128 * d) == 0:
            best = d
    return best


def kernel(
    n, ns, size, steps,
    traj_in, targ_in, reac_in, guess_in, out_ref,
    traj, targ, reac, coef, src, spread, arate, x0, x0h, x1, x1h, packs, packr,
    c1, res, ga, gr, ppa, pp, rpa, rp, es, e, eh, fine,
    load_sem, out_sem, send_sem, recv_sem,
):
    factor, rows, cols = traj.shape
    quarter = cols // size
    groups = n // size
    ext = rows + EDGE
    half = EDGE // 2
    t, s = lax.axis_index("tm"), lax.axis_index("space")
    m, g = lax.rem(t, size), lax.div(t, size)
    base = g * size
    has_up, has_down = s > 0, s < ns - 1
    has_prev, has_next = t > 0, t < n - 1
    both = jnp.logical_and

    loads = [
        pltpu.make_async_copy(a, b, load_sem.at[i])
        for i, (a, b) in enumerate([(traj_in, traj), (reac_in, reac), (targ_in, targ)])
    ]
    for copy in loads:
        copy.start()

    def clear(condition, *refs):
        @pl.when(condition)
        def _():
            for ref in refs:
                ref[...] = jnp.zeros(ref.shape, ref.dtype)

    clear(jnp.logical_not(has_next), x0, x1)
    clear(jnp.logical_not(both(has_next, has_down)), x0h.at[0], x1h.at[0])
    clear(jnp.logical_not(both(has_next, has_up)), x0h.at[1], x1h.at[1])
    clear(jnp.logical_not(has_down), eh.at[0], *[packr.at[i, 0] for i in range(factor - 1)])
    clear(jnp.logical_not(has_up), eh.at[1], *[packr.at[i, 1] for i in range(factor - 1)])
    for d in range(1, groups):
        clear(g + d >= groups, rp.at[d], rpa.at[d])

    barrier = pltpu.get_barrier_semaphore()
    greeted = jnp.int32(0)

    def greet(condition, device):
        @pl.when(condition)
        def _():
            pl.semaphore_signal(barrier, inc=1, device_id=device, device_id_type=MESH)

        return jnp.where(condition, 1, 0).astype(jnp.int32)

    always = s >= 0
    for ds, here in ((0, always), (-1, has_up), (1, has_down)):
        greeted += greet(both(has_prev, here), (t - 1, s + ds))
        greeted += greet(both(has_next, here), (t + 1, s + ds))
        if ds:
            greeted += greet(here, (t, s + ds))
        for d in range(1, size):
            greeted += greet(here, (base + lax.rem(m + d, size), s + ds))
    for d in range(1, groups):
        greeted += greet(g - d >= 0, (t - d * size, s))
        greeted += greet(g + d < groups, (t + d * size, s))

    counter = [0]
    sent = []

    class Move:
        def __init__(self, source, target, device, sends, receives):
            k = counter[0]
            counter[0] += 1
            self.copy = pltpu.make_async_remote_copy(
                src_ref=source, dst_ref=target, send_sem=send_sem.at[k],
                recv_sem=recv_sem.at[k], device_id=device, device_id_type=MESH,
            )
            self.sends, self.receives = sends, receives
            sent.append(self)

        def start(self):
            pl.when(self.sends)(lambda: self.copy.start())

        def landed(self):
            pl.when(self.receives)(lambda: self.copy.wait_recv())

        def left(self):
            pl.when(self.sends)(lambda: self.copy.wait_send())

    top, bottom = pl.ds(0, EDGE), pl.ds(rows - EDGE, EDGE)

    def to_previous(source, x, xh):
        return [
            Move(source.at[top], xh.at[0], (t - 1, s - 1), both(has_prev, has_up), both(has_next, has_down)),
            Move(source.at[bottom], xh.at[1], (t - 1, s + 1), both(has_prev, has_down), both(has_next, has_up)),
            Move(source, x, (t - 1, s), has_prev, has_next),
        ]

    def part(k):
        return pl.ds(pl.multiple_of(k * quarter, quarter), quarter)

    def member(d):
        return lax.rem(m + d, size)

    pl.semaphore_wait(barrier, greeted)
    first = to_previous(guess_in.at[0], x0, x0h)
    for move in first:
        move.start()

    for copy in loads:
        copy.wait()

    sub = lax.broadcasted_iota(jnp.int32, (EDGE, cols), 0) < half

    def halo(from_below, from_above):
        return jnp.where(sub, from_below, from_above)

    reaction = reac[...]
    target = targ[...]
    rates = [None] * factor
    strips = []
    for i in range(factor - 1, -1, -1):
        state = traj[i].astype(jnp.float32)
        rates[i] = reaction * (1.0 - 2.0 * state)
        c = (1.0 - 4.0 * DIFFUSION) + rates[i]
        q = (state - target) * (1.0 / steps)
        coef[i, :rows] = c
        src[i, :rows] = q
        if i:
            packs[i - 1, 0] = jnp.where(sub, c[:EDGE], pltpu.roll(q[:EDGE], half, 0))
            packs[i - 1, 1] = jnp.where(sub, pltpu.roll(q[rows - EDGE :], half, 0), c[rows - EDGE :])
            pair = [
                Move(packs.at[i - 1, 0], packr.at[i - 1, 0], (t, s - 1), has_up, has_down),
                Move(packs.at[i - 1, 1], packr.at[i - 1, 1], (t, s + 1), has_down, has_up),
            ]
            for move in pair:
                move.start()
            strips.append((i, pair))
        else:
            coef[i, rows:] = jnp.zeros((EDGE, cols), jnp.float32)
            src[i, rows:] = jnp.zeros((EDGE, cols), jnp.float32)
    product = 1.0 + rates[0]
    for i in range(1, factor):
        product = product * (1.0 + rates[i])
    arate[...] = product
    below = jnp.where(has_down, DIFFUSION, 0.0).astype(jnp.float32)
    above = jnp.where(has_up, DIFFUSION, 0.0).astype(jnp.float32)
    spread[...] = jnp.where(sub, below, above)

    for i, pair in strips:
        for move in pair:
            move.landed()
        b, a = packr[i - 1, 0], packr[i - 1, 1]
        coef[i, rows:] = halo(b, a)
        src[i, rows:] = pltpu.roll(halo(a, b), half, 0)

    column = lax.broadcasted_iota(jnp.int32, (ext, cols), 1)

    def advance(v, i):
        around = pltpu.roll(v, 1, 0) + pltpu.roll(v, ext - 1, 0)
        around = around + jnp.where(column == 0, 0.0, pltpu.roll(v, 1, 1))
        around = around + jnp.where(column == cols - 1, 0.0, pltpu.roll(v, cols - 1, 1))
        scaled = jnp.concatenate([DIFFUSION * around[:rows], spread[...] * around[rows:]], 0)
        return coef[i] * v + scaled + src[i]

    def relax(v):
        for i in range(factor - 1, -1, -1):
            v = advance(v, i)
        return v[:rows]

    for move in first:
        move.landed()
    centre = relax(jnp.concatenate([x0[...], halo(x0h[0], x0h[1])], 0))
    c1[...] = centre
    second = to_previous(c1, x1, x1h)
    for move in second:
        move.start()

    def transpose(source, target):
        moves = [
            Move(source.at[:, part(member(d))], target.at[m], (base + member(d), s), always, always)
            for d in range(1, size)
        ]
        for move in moves:
            move.start()
        target[m] = source[:, part(m)]
        return moves

    a_moves = transpose(arate, ga)

    for move in second:
        move.landed()
    centre = relax(jnp.concatenate([x1[...], halo(x1h[0], x1h[1])], 0))
    res[...] = centre - c1[...]
    r_moves = transpose(res, gr)

    def to_lower(source, target):
        moves = [
            Move(source, target.at[d], (t - d * size, s), g - d >= 0, g + d < groups)
            for d in range(groups - 1, 0, -1)
        ]
        for move in moves:
            move.start()
        return moves

    for move in a_moves:
        move.landed()
    value = ga[0]
    for k in range(1, size):
        value = value * ga[k]
    ppa[...] = value
    pa_moves = to_lower(ppa, rpa)

    for move in r_moves:
        move.landed()
    value = gr[size - 1]
    for k in range(size - 2, -1, -1):
        value = ga[k] * value + gr[k]
    pp[...] = value
    p_moves = to_lower(pp, rp)
    for move in pa_moves:
        move.landed()
    for move in p_moves:
        move.landed()

    value = rp[groups - 1]
    for d in range(groups - 2, 0, -1):
        value = rp[d] + rpa[d] * value
    es[size - 1] = value
    for k in range(size - 1, 0, -1):
        value = ga[k] * value + gr[k]
        es[k - 1] = value
    e_moves = []
    for d in range(size - 1, -1, -1):
        k = member(d)
        to = base + k
        moves = [
            Move(es.at[k, top], eh.at[0, :, part(m)], (to, s - 1), has_up, has_down),
            Move(es.at[k, bottom], eh.at[1, :, part(m)], (to, s + 1), has_down, has_up),
        ]
        if d:
            moves.append(Move(es.at[k], e.at[:, part(m)], (to, s), always, always))
        for move in moves:
            move.start()
        e_moves += moves
    e[:, part(m)] = es[m]
    for move in e_moves:
        move.landed()

    entering = e[...]
    fine[0] = c1[...] + (arate[...] * entering + res[...])
    outs = [pltpu.make_async_copy(fine.at[i], out_ref.at[i], out_sem.at[i]) for i in range(factor)]
    outs[0].start()
    v = jnp.concatenate([x1[...] + entering, halo(x1h[0], x1h[1]) + halo(eh[0], eh[1])], 0)
    for i in range(factor - 1, 0, -1):
        v = advance(v, i)
        fine[i] = v[:rows]
        outs[i].start()
    for copy in outs:
        copy.wait()
    for move in sent:
        move.left()


def local(trajectory, target, reaction, guess):
    factor, rows, cols = trajectory.shape
    assert guess.shape[0] == 1
    n, ns = lax.axis_size("tm"), lax.axis_size("space")
    size = group_size(n, cols)
    groups = n // size
    quarter = cols // size
    ext = rows + EDGE
    copies = 6 + 2 * (factor - 1) + 2 * (size - 1) + 2 * (groups - 1) + 3 * size - 1
    f32 = jnp.float32
    vmem = lambda *shape: pltpu.VMEM(shape, f32)
    anywhere = pl.BlockSpec(memory_space=pl.ANY)
    return pl.pallas_call(
        functools.partial(kernel, n, ns, size, float(factor * n)),
        out_shape=jax.ShapeDtypeStruct((factor, rows, cols), f32),
        in_specs=[anywhere] * 4,
        out_specs=anywhere,
        scratch_shapes=[
            pltpu.VMEM((factor, rows, cols), trajectory.dtype),
            vmem(rows, cols), vmem(rows, cols),
            vmem(factor, ext, cols), vmem(factor, ext, cols), vmem(EDGE, cols),
            vmem(rows, cols),
            vmem(rows, cols), vmem(2, EDGE, cols), vmem(rows, cols), vmem(2, EDGE, cols),
            vmem(factor - 1, 2, EDGE, cols), vmem(factor - 1, 2, EDGE, cols),
            vmem(rows, cols), vmem(rows, cols),
            vmem(size, rows, quarter), vmem(size, rows, quarter),
            vmem(rows, quarter), vmem(rows, quarter),
            vmem(groups, rows, quarter), vmem(groups, rows, quarter),
            vmem(size, rows, quarter), vmem(rows, cols), vmem(2, EDGE, cols),
            vmem(factor, rows, cols),
            pltpu.SemaphoreType.DMA((3,)), pltpu.SemaphoreType.DMA((factor,)),
            pltpu.SemaphoreType.DMA((copies,)), pltpu.SemaphoreType.DMA((copies,)),
        ],
        compiler_params=pltpu.CompilerParams(collective_id=0, has_side_effects=True),
    )(trajectory, target, reaction, guess)


def solution(mesh):
    in_specs = (P("tm", "space", None), P("space", None), P("space", None), P("tm", "space", None))
    out_specs = P("tm", "space", None)
    return jax.shard_map(local, mesh=mesh, in_specs=in_specs, out_specs=out_specs, check_vma=False)
```

```python
import functools
import jax
import jax.numpy as jnp
from jax import lax
from jax.experimental import pallas as pl
from jax.experimental.pallas import tpu as pltpu
from jax.sharding import PartitionSpec as P

DIFFUSION = 0.05
MESH = pl.DeviceIdType.MESH
EDGE = 8


def group_size(count, cols):
    best = 1
    for d in range(1, count + 1):
        if d * d <= count and count % d == 0 and cols % (128 * d) == 0:
            best = d
    return best


def kernel(
    n, ns, size, steps,
    traj_in, targ_in, reac_in, guess_in, out_ref,
    traj, targ, reac, coef, src, spread, arate, x0, x0h, x1, x1h, packs, packr,
    c1, res, ga, gr, ppa, pp, rpa, rp, es, e, eh, fine,
    load_sem, out_sem, send_sem, recv_sem,
):
    factor, rows, cols = traj.shape
    quarter = cols // size
    groups = n // size
    ext = rows + EDGE
    half = EDGE // 2
    t, s = lax.axis_index("tm"), lax.axis_index("space")
    m, g = lax.rem(t, size), lax.div(t, size)
    base = g * size
    has_up, has_down = s > 0, s < ns - 1
    has_prev, has_next = t > 0, t < n - 1
    both = jnp.logical_and

    loads = [
        pltpu.make_async_copy(a, b, load_sem.at[i])
        for i, (a, b) in enumerate([(traj_in, traj), (reac_in, reac), (targ_in, targ)])
    ]
    for copy in loads:
        copy.start()

    def clear(condition, *refs):
        @pl.when(condition)
        def _():
            for ref in refs:
                ref[...] = jnp.zeros(ref.shape, ref.dtype)

    clear(jnp.logical_not(has_next), x0, x1)
    clear(jnp.logical_not(both(has_next, has_down)), x0h.at[0], x1h.at[0])
    clear(jnp.logical_not(both(has_next, has_up)), x0h.at[1], x1h.at[1])
    clear(jnp.logical_not(has_down), eh.at[0], *[packr.at[i, 0] for i in range(factor - 1)])
    clear(jnp.logical_not(has_up), eh.at[1], *[packr.at[i, 1] for i in range(factor - 1)])
    for d in range(1, groups):
        clear(g + d >= groups, rp.at[d], rpa.at[d])

    barrier = pltpu.get_barrier_semaphore()
    greeted = jnp.int32(0)

    def greet(condition, device):
        @pl.when(condition)
        def _():
            pl.semaphore_signal(barrier, inc=1, device_id=device, device_id_type=MESH)

        return jnp.where(condition, 1, 0).astype(jnp.int32)

    always = s >= 0
    for ds, here in ((0, always), (-1, has_up), (1, has_down)):
        greeted += greet(both(has_prev, here), (t - 1, s + ds))
        greeted += greet(both(has_next, here), (t + 1, s + ds))
        if ds:
            greeted += greet(here, (t, s + ds))
        for d in range(1, size):
            greeted += greet(here, (base + lax.rem(m + d, size), s + ds))
    for d in range(1, groups):
        greeted += greet(g - d >= 0, (t - d * size, s))
        greeted += greet(g + d < groups, (t + d * size, s))

    counter = [0]
    sent = []

    class Move:
        def __init__(self, source, target, device, sends, receives):
            k = counter[0]
            counter[0] += 1
            self.copy = pltpu.make_async_remote_copy(
                src_ref=source, dst_ref=target, send_sem=send_sem.at[k],
                recv_sem=recv_sem.at[k], device_id=device, device_id_type=MESH,
            )
            self.sends, self.receives = sends, receives
            sent.append(self)

        def start(self):
            pl.when(self.sends)(lambda: self.copy.start())

        def landed(self):
            pl.when(self.receives)(lambda: self.copy.wait_recv())

        def left(self):
            pl.when(self.sends)(lambda: self.copy.wait_send())

    top, bottom = pl.ds(0, EDGE), pl.ds(rows - EDGE, EDGE)

    def to_previous(source, x, xh):
        return [
            Move(source.at[top], xh.at[0], (t - 1, s - 1), both(has_prev, has_up), both(has_next, has_down)),
            Move(source.at[bottom], xh.at[1], (t - 1, s + 1), both(has_prev, has_down), both(has_next, has_up)),
            Move(source, x, (t - 1, s), has_prev, has_next),
        ]

    def split(ref, value):
        for k in range(size):
            ref[k] = value[:, k * quarter : (k + 1) * quarter]

    def joined(ref, *lead):
        return jnp.concatenate([ref[(*lead, k)] for k in range(size)], 1)

    def member(d):
        return lax.rem(m + d, size)

    def transpose(source, target):
        moves = [
            Move(source.at[member(d)], target.at[m], (base + member(d), s), always, always)
            for d in range(1, size)
        ]
        for move in moves:
            move.start()
        target[m] = source[m]
        return moves

    pl.semaphore_wait(barrier, greeted)
    first = to_previous(guess_in.at[0], x0, x0h)
    for move in first:
        move.start()

    for copy in loads:
        copy.wait()

    sub = lax.broadcasted_iota(jnp.int32, (EDGE, cols), 0) < half

    def halo(from_below, from_above):
        return jnp.where(sub, from_below, from_above)

    reaction = reac[...]
    target = targ[...]
    rates = [None] * factor
    strips = []
    for i in range(factor - 1, -1, -1):
        state = traj[i].astype(jnp.float32)
        rates[i] = reaction * (1.0 - 2.0 * state)
        c = (1.0 - 4.0 * DIFFUSION) + rates[i]
        q = (state - target) * (1.0 / steps)
        coef[i, :rows] = c
        src[i, :rows] = q
        if i:
            packs[i - 1, 0] = jnp.where(sub, c[:EDGE], pltpu.roll(q[:EDGE], half, 0))
            packs[i - 1, 1] = jnp.where(sub, pltpu.roll(q[rows - EDGE :], half, 0), c[rows - EDGE :])
            pair = [
                Move(packs.at[i - 1, 0], packr.at[i - 1, 0], (t, s - 1), has_up, has_down),
                Move(packs.at[i - 1, 1], packr.at[i - 1, 1], (t, s + 1), has_down, has_up),
            ]
            for move in pair:
                move.start()
            strips.append((i, pair))
        else:
            coef[i, rows:] = jnp.zeros((EDGE, cols), jnp.float32)
            src[i, rows:] = jnp.zeros((EDGE, cols), jnp.float32)
    product = 1.0 + rates[0]
    for i in range(1, factor):
        product = product * (1.0 + rates[i])
    split(arate, product)
    a_moves = transpose(arate, ga)
    below = jnp.where(has_down, DIFFUSION, 0.0).astype(jnp.float32)
    above = jnp.where(has_up, DIFFUSION, 0.0).astype(jnp.float32)
    spread[...] = jnp.where(sub, below, above)

    for i, pair in strips:
        for move in pair:
            move.landed()
        b, a = packr[i - 1, 0], packr[i - 1, 1]
        coef[i, rows:] = halo(b, a)
        src[i, rows:] = pltpu.roll(halo(a, b), half, 0)

    column = lax.broadcasted_iota(jnp.int32, (ext, cols), 1)

    def advance(v, i):
        around = pltpu.roll(v, 1, 0) + pltpu.roll(v, ext - 1, 0)
        around = around + jnp.where(column == 0, 0.0, pltpu.roll(v, 1, 1))
        around = around + jnp.where(column == cols - 1, 0.0, pltpu.roll(v, cols - 1, 1))
        scaled = jnp.concatenate([DIFFUSION * around[:rows], spread[...] * around[rows:]], 0)
        return coef[i] * v + scaled + src[i]

    def relax(v):
        for i in range(factor - 1, -1, -1):
            v = advance(v, i)
        return v[:rows]

    for move in first:
        move.landed()
    centre = relax(jnp.concatenate([x0[...], halo(x0h[0], x0h[1])], 0))
    c1[...] = centre
    second = to_previous(c1, x1, x1h)
    for move in second:
        move.start()

    for move in second:
        move.landed()
    centre = relax(jnp.concatenate([x1[...], halo(x1h[0], x1h[1])], 0))
    split(res, centre - c1[...])
    r_moves = transpose(res, gr)

    def to_lower(source, target):
        moves = [
            Move(source, target.at[d], (t - d * size, s), g - d >= 0, g + d < groups)
            for d in range(groups - 1, 0, -1)
        ]
        for move in moves:
            move.start()
        return moves

    for move in a_moves:
        move.landed()
    value = ga[0]
    for k in range(1, size):
        value = value * ga[k]
    ppa[...] = value
    pa_moves = to_lower(ppa, rpa)

    for move in r_moves:
        move.landed()
    value = gr[size - 1]
    for k in range(size - 2, -1, -1):
        value = ga[k] * value + gr[k]
    pp[...] = value
    p_moves = to_lower(pp, rp)
    for move in pa_moves:
        move.landed()
    for move in p_moves:
        move.landed()

    value = rp[groups - 1]
    for d in range(groups - 2, 0, -1):
        value = rp[d] + rpa[d] * value
    es[size - 1] = value
    for k in range(size - 1, 0, -1):
        value = ga[k] * value + gr[k]
        es[k - 1] = value
    e_moves = []
    for d in range(size - 1, -1, -1):
        k = member(d)
        to = base + k
        moves = [
            Move(es.at[k, top], eh.at[0, m], (to, s - 1), has_up, has_down),
            Move(es.at[k, bottom], eh.at[1, m], (to, s + 1), has_down, has_up),
        ]
        if d:
            moves.append(Move(es.at[k], e.at[m], (to, s), always, always))
        for move in moves:
            move.start()
        e_moves += moves
    e[m] = es[m]
    for move in e_moves:
        move.landed()

    entering = joined(e)
    fine[0] = c1[...] + (joined(arate) * entering + joined(res))
    outs = [pltpu.make_async_copy(fine.at[i], out_ref.at[i], out_sem.at[i]) for i in range(factor)]
    outs[0].start()
    v = jnp.concatenate([x1[...] + entering, halo(x1h[0], x1h[1]) + halo(joined(eh, 0), joined(eh, 1))], 0)
    for i in range(factor - 1, 0, -1):
        v = advance(v, i)
        fine[i] = v[:rows]
        outs[i].start()
    for copy in outs:
        copy.wait()
    for move in sent:
        move.left()


def local(trajectory, target, reaction, guess):
    factor, rows, cols = trajectory.shape
    assert guess.shape[0] == 1
    n, ns = lax.axis_size("tm"), lax.axis_size("space")
    size = group_size(n, cols)
    groups = n // size
    quarter = cols // size
    ext = rows + EDGE
    copies = 6 + 2 * (factor - 1) + 2 * (size - 1) + 2 * (groups - 1) + 3 * size - 1
    f32 = jnp.float32
    vmem = lambda *shape: pltpu.VMEM(shape, f32)
    anywhere = pl.BlockSpec(memory_space=pl.ANY)
    return pl.pallas_call(
        functools.partial(kernel, n, ns, size, float(factor * n)),
        out_shape=jax.ShapeDtypeStruct((factor, rows, cols), f32),
        in_specs=[anywhere] * 4,
        out_specs=anywhere,
        scratch_shapes=[
            pltpu.VMEM((factor, rows, cols), trajectory.dtype),
            vmem(rows, cols), vmem(rows, cols),
            vmem(factor, ext, cols), vmem(factor, ext, cols), vmem(EDGE, cols),
            vmem(size, rows, quarter),
            vmem(rows, cols), vmem(2, EDGE, cols), vmem(rows, cols), vmem(2, EDGE, cols),
            vmem(factor - 1, 2, EDGE, cols), vmem(factor - 1, 2, EDGE, cols),
            vmem(rows, cols), vmem(size, rows, quarter),
            vmem(size, rows, quarter), vmem(size, rows, quarter),
            vmem(rows, quarter), vmem(rows, quarter),
            vmem(groups, rows, quarter), vmem(groups, rows, quarter),
            vmem(size, rows, quarter), vmem(size, rows, quarter), vmem(2, size, EDGE, quarter),
            vmem(factor, rows, cols),
            pltpu.SemaphoreType.DMA((3,)), pltpu.SemaphoreType.DMA((factor,)),
            pltpu.SemaphoreType.DMA((copies,)), pltpu.SemaphoreType.DMA((copies,)),
        ],
        compiler_params=pltpu.CompilerParams(collective_id=0, has_side_effects=True),
    )(trajectory, target, reaction, guess)


def solution(mesh):
    in_specs = (P("tm", "space", None), P("space", None), P("space", None), P("tm", "space", None))
    out_specs = P("tm", "space", None)
    return jax.shard_map(local, mesh=mesh, in_specs=in_specs, out_specs=out_specs, check_vma=False)
```

```python
import functools
import jax
import jax.numpy as jnp
from jax import lax
from jax.experimental import pallas as pl
from jax.experimental.pallas import tpu as pltpu
from jax.sharding import PartitionSpec as P

DIFFUSION = 0.05
MESH = pl.DeviceIdType.MESH
EDGE = 8


def group_size(count, cols):
    best = 1
    for d in range(1, count + 1):
        if d * d <= count and count % d == 0 and cols % (128 * d) == 0:
            best = d
    return best


def kernel(
    n, ns, size, steps,
    traj_in, targ_in, reac_in, guess_in, out_ref,
    traj, targ, reac, coef, src, spread, arate, x0, x0h, x1, x1h, packs, packr,
    c1, res, ga, gr, ppa, pp, rpa, rp, es, e, eh, fine,
    load_sem, out_sem, send_sem, recv_sem, lower_sem,
):
    factor, rows, cols = traj.shape
    quarter = cols // size
    groups = n // size
    ext = rows + EDGE
    half = EDGE // 2
    t, s = lax.axis_index("tm"), lax.axis_index("space")
    m, g = lax.rem(t, size), lax.div(t, size)
    base = g * size
    has_up, has_down = s > 0, s < ns - 1
    has_prev, has_next = t > 0, t < n - 1
    both = jnp.logical_and

    loads = [
        pltpu.make_async_copy(a, b, load_sem.at[i])
        for i, (a, b) in enumerate([(traj_in, traj), (reac_in, reac), (targ_in, targ)])
    ]
    for copy in loads:
        copy.start()

    def clear(condition, *refs):
        @pl.when(condition)
        def _():
            for ref in refs:
                ref[...] = jnp.zeros(ref.shape, ref.dtype)

    clear(jnp.logical_not(has_next), x0, x1)
    clear(jnp.logical_not(both(has_next, has_down)), x0h.at[0], x1h.at[0])
    clear(jnp.logical_not(both(has_next, has_up)), x0h.at[1], x1h.at[1])
    clear(jnp.logical_not(has_down), eh.at[0], *[packr.at[i, 0] for i in range(factor - 1)])
    clear(jnp.logical_not(has_up), eh.at[1], *[packr.at[i, 1] for i in range(factor - 1)])
    for d in range(1, groups):
        clear(g + d >= groups, rp.at[d], rpa.at[d])

    barrier = pltpu.get_barrier_semaphore()
    greeted = jnp.int32(0)

    def greet(condition, device):
        @pl.when(condition)
        def _():
            pl.semaphore_signal(barrier, inc=1, device_id=device, device_id_type=MESH)

        return jnp.where(condition, 1, 0).astype(jnp.int32)

    always = s >= 0
    for ds, here in ((0, always), (-1, has_up), (1, has_down)):
        greeted += greet(both(has_prev, here), (t - 1, s + ds))
        greeted += greet(both(has_next, here), (t + 1, s + ds))
        if ds:
            greeted += greet(here, (t, s + ds))
        for d in range(1, size):
            greeted += greet(here, (base + lax.rem(m + d, size), s + ds))
    greeted += greet(g > 0, (t - size, s))
    greeted += greet(g + 1 < groups, (t + size, s))

    counter = [0]
    sent = []

    class Move:
        def __init__(self, source, target, device, sends, receives):
            k = counter[0]
            counter[0] += 1
            self.copy = pltpu.make_async_remote_copy(
                src_ref=source, dst_ref=target, send_sem=send_sem.at[k],
                recv_sem=recv_sem.at[k], device_id=device, device_id_type=MESH,
            )
            self.sends, self.receives = sends, receives
            sent.append(self)

        def start(self):
            pl.when(self.sends)(lambda: self.copy.start())

        def landed(self):
            pl.when(self.receives)(lambda: self.copy.wait_recv())

        def left(self):
            pl.when(self.sends)(lambda: self.copy.wait_send())

    top, bottom = pl.ds(0, EDGE), pl.ds(rows - EDGE, EDGE)

    def to_previous(source, x, xh):
        return [
            Move(source.at[top], xh.at[0], (t - 1, s - 1), both(has_prev, has_up), both(has_next, has_down)),
            Move(source.at[bottom], xh.at[1], (t - 1, s + 1), both(has_prev, has_down), both(has_next, has_up)),
            Move(source, x, (t - 1, s), has_prev, has_next),
        ]

    def split(ref, value):
        for k in range(size):
            ref[k] = value[:, k * quarter : (k + 1) * quarter]

    def joined(ref, *lead):
        return jnp.concatenate([ref[(*lead, k)] for k in range(size)], 1)

    def member(d):
        return lax.rem(m + d, size)

    whole = pl.ds(0, rows)

    def transpose(source, target, strip):
        moves = [
            Move(source.at[member(d), strip], target.at[m, strip], (base + member(d), s), always, always)
            for d in range(1, size)
        ]
        for move in moves:
            move.start()
        return moves

    pl.semaphore_wait(barrier, greeted)
    first = to_previous(guess_in.at[0], x0, x0h)
    for move in first:
        move.start()

    for copy in loads:
        copy.wait()

    sub = lax.broadcasted_iota(jnp.int32, (EDGE, cols), 0) < half

    def halo(from_below, from_above):
        return jnp.where(sub, from_below, from_above)

    reaction = reac[...]
    target = targ[...]
    rates = [None] * factor
    strips = []
    for i in range(factor - 1, -1, -1):
        state = traj[i].astype(jnp.float32)
        rates[i] = reaction * (1.0 - 2.0 * state)
        c = (1.0 - 4.0 * DIFFUSION) + rates[i]
        q = (state - target) * (1.0 / steps)
        coef[i, :rows] = c
        src[i, :rows] = q
        if i:
            packs[i - 1, 0] = jnp.where(sub, c[:EDGE], pltpu.roll(q[:EDGE], half, 0))
            packs[i - 1, 1] = jnp.where(sub, pltpu.roll(q[rows - EDGE :], half, 0), c[rows - EDGE :])
            pair = [
                Move(packs.at[i - 1, 0], packr.at[i - 1, 0], (t, s - 1), has_up, has_down),
                Move(packs.at[i - 1, 1], packr.at[i - 1, 1], (t, s + 1), has_down, has_up),
            ]
            for move in pair:
                move.start()
            strips.append((i, pair))
        else:
            coef[i, rows:] = jnp.zeros((EDGE, cols), jnp.float32)
            src[i, rows:] = jnp.zeros((EDGE, cols), jnp.float32)
    product = 1.0 + rates[0]
    for i in range(1, factor):
        product = product * (1.0 + rates[i])
    split(arate, product)
    a_moves = transpose(arate, ga, whole)
    ga[m] = arate[m]
    below = jnp.where(has_down, DIFFUSION, 0.0).astype(jnp.float32)
    above = jnp.where(has_up, DIFFUSION, 0.0).astype(jnp.float32)
    spread[...] = jnp.where(sub, below, above)

    for i, pair in strips:
        for move in pair:
            move.landed()
        b, a = packr[i - 1, 0], packr[i - 1, 1]
        coef[i, rows:] = halo(b, a)
        src[i, rows:] = pltpu.roll(halo(a, b), half, 0)

    column = lax.broadcasted_iota(jnp.int32, (ext, cols), 1)

    def advance(v, i):
        around = pltpu.roll(v, 1, 0) + pltpu.roll(v, ext - 1, 0)
        around = around + jnp.where(column == 0, 0.0, pltpu.roll(v, 1, 1))
        around = around + jnp.where(column == cols - 1, 0.0, pltpu.roll(v, cols - 1, 1))
        scaled = jnp.concatenate([DIFFUSION * around[:rows], spread[...] * around[rows:]], 0)
        return coef[i] * v + scaled + src[i]

    def relax(v):
        for i in range(factor - 1, -1, -1):
            v = advance(v, i)
        return v[:rows]

    for move in first:
        move.landed()
    centre = relax(jnp.concatenate([x0[...], halo(x0h[0], x0h[1])], 0))
    c1[...] = centre
    second = to_previous(c1, x1, x1h)
    for move in second:
        move.start()

    @pl.when(g > 1)
    def _():
        pl.semaphore_wait(lower_sem, 1)

    @pl.when(both(g > 0, g + 1 < groups))
    def _():
        pl.semaphore_signal(lower_sem, inc=1, device_id=(t + size, s), device_id_type=MESH)

    for move in second:
        move.landed()
    centre = relax(jnp.concatenate([x1[...], halo(x1h[0], x1h[1])], 0))
    split(res, centre - c1[...])
    count = rows // EDGE
    chunks = [0, count - 1] + list(range(1, count - 1)) if count > 1 else [0]
    strip = {c: pl.ds(c * EDGE, EDGE) for c in chunks}
    r_moves = {c: transpose(res, gr, strip[c]) for c in chunks}
    gr[m] = res[m]

    def to_lower(source, target, strip):
        moves = [
            Move(source.at[strip], target.at[d, strip], (t - d * size, s), g - d >= 0, g + d < groups)
            for d in range(groups - 1, 0, -1)
        ]
        for move in moves:
            move.start()
        return moves

    for move in a_moves:
        move.landed()
    value = ga[0]
    for k in range(1, size):
        value = value * ga[k]
    ppa[...] = value
    pa_moves = to_lower(ppa, rpa, whole)

    p_moves = {}
    for c in chunks:
        for move in r_moves[c]:
            move.landed()
        value = gr[size - 1, strip[c]]
        for k in range(size - 2, -1, -1):
            value = ga[k, strip[c]] * value + gr[k, strip[c]]
        pp[strip[c]] = value
        p_moves[c] = to_lower(pp, rp, strip[c])
    for move in pa_moves:
        move.landed()

    e_moves = []
    for c in chunks:
        for move in p_moves[c]:
            move.landed()
        value = rp[groups - 1, strip[c]]
        for d in range(groups - 2, 0, -1):
            value = rp[d, strip[c]] + rpa[d, strip[c]] * value
        es[size - 1, strip[c]] = value
        for k in range(size - 1, 0, -1):
            value = ga[k, strip[c]] * value + gr[k, strip[c]]
            es[k - 1, strip[c]] = value
        for d in range(size):
            k = member(d)
            to = base + k
            moves = []
            if c == 0:
                moves.append(Move(es.at[k, top], eh.at[0, m], (to, s - 1), has_up, has_down))
            if c == count - 1:
                moves.append(Move(es.at[k, bottom], eh.at[1, m], (to, s + 1), has_down, has_up))
            if d:
                moves.append(Move(es.at[k, strip[c]], e.at[m, strip[c]], (to, s), always, always))
            for move in moves:
                move.start()
            e_moves += moves
    e[m] = es[m]
    for move in e_moves:
        move.landed()

    entering = joined(e)
    fine[0] = c1[...] + (joined(arate) * entering + joined(res))
    outs = [pltpu.make_async_copy(fine.at[i], out_ref.at[i], out_sem.at[i]) for i in range(factor)]
    outs[0].start()
    v = jnp.concatenate([x1[...] + entering, halo(x1h[0], x1h[1]) + halo(joined(eh, 0), joined(eh, 1))], 0)
    for i in range(factor - 1, 0, -1):
        v = advance(v, i)
        fine[i] = v[:rows]
        outs[i].start()
    for copy in outs:
        copy.wait()
    for move in sent:
        move.left()


def local(trajectory, target, reaction, guess):
    factor, rows, cols = trajectory.shape
    assert guess.shape[0] == 1
    n, ns = lax.axis_size("tm"), lax.axis_size("space")
    size = group_size(n, cols)
    groups = n // size
    quarter = cols // size
    ext = rows + EDGE
    count = rows // EDGE
    copies = 6 + 2 * (factor - 1) + (2 * count + 1) * (size - 1) + (count + 1) * (groups - 1) + 2 * size
    f32 = jnp.float32
    vmem = lambda *shape: pltpu.VMEM(shape, f32)
    anywhere = pl.BlockSpec(memory_space=pl.ANY)
    return pl.pallas_call(
        functools.partial(kernel, n, ns, size, float(factor * n)),
        out_shape=jax.ShapeDtypeStruct((factor, rows, cols), f32),
        in_specs=[anywhere] * 4,
        out_specs=anywhere,
        scratch_shapes=[
            pltpu.VMEM((factor, rows, cols), trajectory.dtype),
            vmem(rows, cols), vmem(rows, cols),
            vmem(factor, ext, cols), vmem(factor, ext, cols), vmem(EDGE, cols),
            vmem(size, rows, quarter),
            vmem(rows, cols), vmem(2, EDGE, cols), vmem(rows, cols), vmem(2, EDGE, cols),
            vmem(factor - 1, 2, EDGE, cols), vmem(factor - 1, 2, EDGE, cols),
            vmem(rows, cols), vmem(size, rows, quarter),
            vmem(size, rows, quarter), vmem(size, rows, quarter),
            vmem(rows, quarter), vmem(rows, quarter),
            vmem(groups, rows, quarter), vmem(groups, rows, quarter),
            vmem(size, rows, quarter), vmem(size, rows, quarter), vmem(2, size, EDGE, quarter),
            vmem(factor, rows, cols),
            pltpu.SemaphoreType.DMA((3,)), pltpu.SemaphoreType.DMA((factor,)),
            pltpu.SemaphoreType.DMA((copies,)), pltpu.SemaphoreType.DMA((copies,)),
            pltpu.SemaphoreType.REGULAR,
        ],
        compiler_params=pltpu.CompilerParams(collective_id=0, has_side_effects=True),
    )(trajectory, target, reaction, guess)


def solution(mesh):
    in_specs = (P("tm", "space", None), P("space", None), P("space", None), P("tm", "space", None))
    out_specs = P("tm", "space", None)
    return jax.shard_map(local, mesh=mesh, in_specs=in_specs, out_specs=out_specs, check_vma=False)
```

```python
import functools
import jax
import jax.numpy as jnp
from jax import lax
from jax.experimental import pallas as pl
from jax.experimental.pallas import tpu as pltpu
from jax.sharding import PartitionSpec as P

DIFFUSION = 0.05
MESH = pl.DeviceIdType.MESH
EDGE = 8


def group_size(count, cols):
    best = 1
    for d in range(1, count + 1):
        if d * d <= count and count % d == 0 and cols % (128 * d) == 0:
            best = d
    return best


def advance(v, i, coef, src, spread):
    ext, cols = v.shape
    rows = ext - EDGE
    column = lax.broadcasted_iota(jnp.int32, (ext, cols), 1)
    around = pltpu.roll(v, 1, 0) + pltpu.roll(v, ext - 1, 0)
    around = around + jnp.where(column == 0, 0.0, pltpu.roll(v, 1, 1))
    around = around + jnp.where(column == cols - 1, 0.0, pltpu.roll(v, cols - 1, 1))
    scaled = jnp.concatenate([DIFFUSION * around[:rows], spread[...] * around[rows:]], 0)
    return coef[i] * v + scaled + src[i]


def finish(coef, src, spread, last, c2, out_ref, fine, out_sem):
    factor, ext, _ = coef.shape
    rows = ext - EDGE
    outs = [
        pltpu.make_async_copy(fine.at[i] if i else c2, out_ref.at[i], out_sem.at[i])
        for i in range(factor)
    ]
    outs[0].start()
    v = last[...]
    for i in range(factor - 1, 0, -1):
        v = advance(v, i, coef, src, spread)
        fine[i] = v[:rows]
        outs[i].start()
    for copy in outs:
        copy.wait()


def kernel(
    n, ns, size, steps,
    traj_in, targ_in, reac_in, guess_in, coef, src, spread, last, c2,
    traj, targ, reac, arate, x0, x0h, x1, x1h, packs, packr,
    c1, res, ga, gr, ppa, pp, rpa, rp, es, e, eh,
    load_sem, send_sem, recv_sem, lower_sem,
):
    factor, rows, cols = traj.shape
    quarter = cols // size
    groups = n // size
    ext = rows + EDGE
    half = EDGE // 2
    t, s = lax.axis_index("tm"), lax.axis_index("space")
    m, g = lax.rem(t, size), lax.div(t, size)
    base = g * size
    has_up, has_down = s > 0, s < ns - 1
    has_prev, has_next = t > 0, t < n - 1
    both = jnp.logical_and

    loads = [
        pltpu.make_async_copy(a, b, load_sem.at[i])
        for i, (a, b) in enumerate([(traj_in, traj), (reac_in, reac), (targ_in, targ)])
    ]
    for copy in loads:
        copy.start()

    def clear(condition, *refs):
        @pl.when(condition)
        def _():
            for ref in refs:
                ref[...] = jnp.zeros(ref.shape, ref.dtype)

    clear(jnp.logical_not(has_next), x0, x1)
    clear(jnp.logical_not(both(has_next, has_down)), x0h.at[0], x1h.at[0])
    clear(jnp.logical_not(both(has_next, has_up)), x0h.at[1], x1h.at[1])
    clear(jnp.logical_not(has_down), eh.at[0], *[packr.at[i, 0] for i in range(factor - 1)])
    clear(jnp.logical_not(has_up), eh.at[1], *[packr.at[i, 1] for i in range(factor - 1)])
    for d in range(1, groups):
        clear(g + d >= groups, rp.at[d], rpa.at[d])

    barrier = pltpu.get_barrier_semaphore()
    greeted = jnp.int32(0)

    def greet(condition, device):
        @pl.when(condition)
        def _():
            pl.semaphore_signal(barrier, inc=1, device_id=device, device_id_type=MESH)

        return jnp.where(condition, 1, 0).astype(jnp.int32)

    always = s >= 0
    for ds, here in ((0, always), (-1, has_up), (1, has_down)):
        greeted += greet(both(has_prev, here), (t - 1, s + ds))
        greeted += greet(both(has_next, here), (t + 1, s + ds))
        if ds:
            greeted += greet(here, (t, s + ds))
        for d in range(1, size):
            greeted += greet(here, (base + lax.rem(m + d, size), s + ds))
    greeted += greet(g > 0, (t - size, s))
    greeted += greet(g + 1 < groups, (t + size, s))

    counter = [0]
    sent = []

    class Move:
        def __init__(self, source, target, device, sends, receives):
            k = counter[0]
            counter[0] += 1
            self.copy = pltpu.make_async_remote_copy(
                src_ref=source, dst_ref=target, send_sem=send_sem.at[k],
                recv_sem=recv_sem.at[k], device_id=device, device_id_type=MESH,
            )
            self.sends, self.receives = sends, receives
            sent.append(self)

        def start(self):
            pl.when(self.sends)(lambda: self.copy.start())

        def landed(self):
            pl.when(self.receives)(lambda: self.copy.wait_recv())

        def left(self):
            pl.when(self.sends)(lambda: self.copy.wait_send())

    top, bottom = pl.ds(0, EDGE), pl.ds(rows - EDGE, EDGE)

    def to_previous(source, x, xh):
        return [
            Move(source.at[top], xh.at[0], (t - 1, s - 1), both(has_prev, has_up), both(has_next, has_down)),
            Move(source.at[bottom], xh.at[1], (t - 1, s + 1), both(has_prev, has_down), both(has_next, has_up)),
            Move(source, x, (t - 1, s), has_prev, has_next),
        ]

    def split(ref, value):
        for k in range(size):
            ref[k] = value[:, k * quarter : (k + 1) * quarter]

    def joined(ref, *lead):
        return jnp.concatenate([ref[(*lead, k)] for k in range(size)], 1)

    def member(d):
        return lax.rem(m + d, size)

    whole = pl.ds(0, rows)

    def transpose(source, target, strip):
        moves = [
            Move(source.at[member(d), strip], target.at[m, strip], (base + member(d), s), always, always)
            for d in range(1, size)
        ]
        for move in moves:
            move.start()
        return moves

    pl.semaphore_wait(barrier, greeted)
    first = to_previous(guess_in.at[0], x0, x0h)
    for move in first:
        move.start()

    for copy in loads:
        copy.wait()

    sub = lax.broadcasted_iota(jnp.int32, (EDGE, cols), 0) < half

    def halo(from_below, from_above):
        return jnp.where(sub, from_below, from_above)

    reaction = reac[...]
    target = targ[...]
    rates = [None] * factor
    strips = []
    for i in range(factor - 1, -1, -1):
        state = traj[i].astype(jnp.float32)
        rates[i] = reaction * (1.0 - 2.0 * state)
        c = (1.0 - 4.0 * DIFFUSION) + rates[i]
        q = (state - target) * (1.0 / steps)
        coef[i, :rows] = c
        src[i, :rows] = q
        if i:
            packs[i - 1, 0] = jnp.where(sub, c[:EDGE], pltpu.roll(q[:EDGE], half, 0))
            packs[i - 1, 1] = jnp.where(sub, pltpu.roll(q[rows - EDGE :], half, 0), c[rows - EDGE :])
            pair = [
                Move(packs.at[i - 1, 0], packr.at[i - 1, 0], (t, s - 1), has_up, has_down),
                Move(packs.at[i - 1, 1], packr.at[i - 1, 1], (t, s + 1), has_down, has_up),
            ]
            for move in pair:
                move.start()
            strips.append((i, pair))
        else:
            coef[i, rows:] = jnp.zeros((EDGE, cols), jnp.float32)
            src[i, rows:] = jnp.zeros((EDGE, cols), jnp.float32)
    product = 1.0 + rates[0]
    for i in range(1, factor):
        product = product * (1.0 + rates[i])
    split(arate, product)
    a_moves = transpose(arate, ga, whole)
    ga[m] = arate[m]
    below = jnp.where(has_down, DIFFUSION, 0.0).astype(jnp.float32)
    above = jnp.where(has_up, DIFFUSION, 0.0).astype(jnp.float32)
    spread[...] = jnp.where(sub, below, above)

    for i, pair in strips:
        for move in pair:
            move.landed()
        b, a = packr[i - 1, 0], packr[i - 1, 1]
        coef[i, rows:] = halo(b, a)
        src[i, rows:] = pltpu.roll(halo(a, b), half, 0)

    def relax(v):
        for i in range(factor - 1, -1, -1):
            v = advance(v, i, coef, src, spread)
        return v[:rows]

    for move in first:
        move.landed()
    centre = relax(jnp.concatenate([x0[...], halo(x0h[0], x0h[1])], 0))
    c1[...] = centre
    second = to_previous(c1, x1, x1h)
    for move in second:
        move.start()

    @pl.when(g > 1)
    def _():
        pl.semaphore_wait(lower_sem, 1)

    @pl.when(both(g > 0, g + 1 < groups))
    def _():
        pl.semaphore_signal(lower_sem, inc=1, device_id=(t + size, s), device_id_type=MESH)

    for move in second:
        move.landed()
    centre = relax(jnp.concatenate([x1[...], halo(x1h[0], x1h[1])], 0))
    split(res, centre - c1[...])
    count = rows // EDGE
    chunks = [0, count - 1] + list(range(1, count - 1)) if count > 1 else [0]
    strip = {c: pl.ds(c * EDGE, EDGE) for c in chunks}
    r_moves = {c: transpose(res, gr, strip[c]) for c in chunks}
    gr[m] = res[m]

    def to_lower(source, target, strip):
        moves = [
            Move(source.at[strip], target.at[d, strip], (t - d * size, s), g - d >= 0, g + d < groups)
            for d in range(groups - 1, 0, -1)
        ]
        for move in moves:
            move.start()
        return moves

    for move in a_moves:
        move.landed()
    value = ga[0]
    for k in range(1, size):
        value = value * ga[k]
    ppa[...] = value
    pa_moves = to_lower(ppa, rpa, whole)

    p_moves = {}
    for c in chunks:
        for move in r_moves[c]:
            move.landed()
        value = gr[size - 1, strip[c]]
        for k in range(size - 2, -1, -1):
            value = ga[k, strip[c]] * value + gr[k, strip[c]]
        pp[strip[c]] = value
        p_moves[c] = to_lower(pp, rp, strip[c])
    for move in pa_moves:
        move.landed()

    e_moves = []
    for c in chunks:
        for move in p_moves[c]:
            move.landed()
        value = rp[groups - 1, strip[c]]
        for d in range(groups - 2, 0, -1):
            value = rp[d, strip[c]] + rpa[d, strip[c]] * value
        es[size - 1, strip[c]] = value
        for k in range(size - 1, 0, -1):
            value = ga[k, strip[c]] * value + gr[k, strip[c]]
            es[k - 1, strip[c]] = value
        for d in range(size):
            k = member(d)
            to = base + k
            moves = []
            if c == 0:
                moves.append(Move(es.at[k, top], eh.at[0, m], (to, s - 1), has_up, has_down))
            if c == count - 1:
                moves.append(Move(es.at[k, bottom], eh.at[1, m], (to, s + 1), has_down, has_up))
            if d:
                moves.append(Move(es.at[k, strip[c]], e.at[m, strip[c]], (to, s), always, always))
            for move in moves:
                move.start()
            e_moves += moves
    e[m] = es[m]
    for move in e_moves:
        move.landed()

    entering = joined(e)
    c2[...] = c1[...] + (joined(arate) * entering + joined(res))
    last[:rows] = x1[...] + entering
    last[rows:] = halo(x1h[0], x1h[1]) + halo(joined(eh, 0), joined(eh, 1))
    for move in sent:
        move.left()


def local(trajectory, target, reaction, guess):
    factor, rows, cols = trajectory.shape
    assert guess.shape[0] == 1
    n, ns = lax.axis_size("tm"), lax.axis_size("space")
    size = group_size(n, cols)
    groups = n // size
    quarter = cols // size
    ext = rows + EDGE
    count = rows // EDGE
    copies = 6 + 2 * (factor - 1) + (2 * count + 1) * (size - 1) + (count + 1) * (groups - 1) + 2 * size
    f32 = jnp.float32
    vmem = lambda *shape: pltpu.VMEM(shape, f32)
    resident = pl.BlockSpec(memory_space=pltpu.VMEM)
    shape = lambda *dims: jax.ShapeDtypeStruct(dims, f32)
    parts = pl.pallas_call(
        functools.partial(kernel, n, ns, size, float(factor * n)),
        out_shape=[
            shape(factor, ext, cols), shape(factor, ext, cols), shape(EDGE, cols),
            shape(ext, cols), shape(rows, cols),
        ],
        in_specs=[pl.BlockSpec(memory_space=pltpu.HBM)] * 4,
        out_specs=[resident] * 5,
        scratch_shapes=[
            pltpu.VMEM((factor, rows, cols), trajectory.dtype),
            vmem(rows, cols), vmem(rows, cols),
            vmem(size, rows, quarter),
            vmem(rows, cols), vmem(2, EDGE, cols), vmem(rows, cols), vmem(2, EDGE, cols),
            vmem(factor - 1, 2, EDGE, cols), vmem(factor - 1, 2, EDGE, cols),
            vmem(rows, cols), vmem(size, rows, quarter),
            vmem(size, rows, quarter), vmem(size, rows, quarter),
            vmem(rows, quarter), vmem(rows, quarter),
            vmem(groups, rows, quarter), vmem(groups, rows, quarter),
            vmem(size, rows, quarter), vmem(size, rows, quarter), vmem(2, size, EDGE, quarter),
            pltpu.SemaphoreType.DMA((3,)),
            pltpu.SemaphoreType.DMA((copies,)), pltpu.SemaphoreType.DMA((copies,)),
            pltpu.SemaphoreType.REGULAR,
        ],
        compiler_params=pltpu.CompilerParams(
            collective_id=0, has_side_effects=True, vmem_limit_bytes=16 << 20
        ),
    )(*[pltpu.with_memory_space_constraint(x, pltpu.HBM) for x in (trajectory, target, reaction, guess)])
    return pl.pallas_call(
        finish,
        out_shape=shape(factor, rows, cols),
        in_specs=[resident] * 5,
        out_specs=pl.BlockSpec(memory_space=pltpu.HBM),
        scratch_shapes=[vmem(factor, rows, cols), pltpu.SemaphoreType.DMA((factor,))],
        compiler_params=pltpu.CompilerParams(vmem_limit_bytes=16 << 20),
    )(*parts)


def solution(mesh):
    in_specs = (P("tm", "space", None), P("space", None), P("space", None), P("tm", "space", None))
    out_specs = P("tm", "space", None)
    return jax.shard_map(local, mesh=mesh, in_specs=in_specs, out_specs=out_specs, check_vma=False)
```
